32 devices in a mesh: wave: 8 (over z, y), lev: 4 (over x, core).
Axes of the slice: x: 2, y: 2, z: 4, core: 2. Of those that a mesh axis runs over, the one named last changes fastest.
Arguments:
- grid_data: float32 [2048, 32, 384], P('wave', None, 'lev'), may hold values from -6 to 6
- legendre: float32 [32, 1024, 1024], P('wave'), may hold values from -0.125 to 0.125
- gauss_weights: float32 [1024], replicated, may hold values from 0.4 to 2
- wave_of_slot: int32 [32], replicated, may hold values from 0 to 31, as said below
- first_tile: int32 [32], P('wave'), may hold values from 0 to 7, as said below
- coupling: float32 [64, 64], P(None, 'lev'), may hold values from -0.75 to 0.75
Outputs:
- grid_out: float32 [2048, 32, 384], P('wave', None, 'lev')
The draws below stay inside these ranges and needn't reach their ends.
Inputs may be any that keep to these rules, and one draw needn't show every extreme that they name: `wave_of_slot`: A permutation of the waves; slots 2q and 2q + 1 hold waves j and 31 - j for some j. `first_tile`: tends to grow with the slot's wavenumber; the slot holding wave 32 - 1 has 7 and the one holding wave 0 has 0.
All inputs are finite; a program needn't handle non-finite values.
Results may differ from the reference program's by a relative error of at most 0.0003.
Values sent between devices are 32-bit elements; how exact they have to be, the bound alone decides.
A program may use at most 128 MiB of HBM per device.

```python
import math
import jax
import jax.numpy as jnp
from jax import lax

NLAT = 2048
NDEG = 1024
TILE = 128
HALF = 1024
TILES = 8
WIN = 32
LEVELS = 64
COLS = 384


def paired_waves(key):
    shuffle = jax.random.permutation(jax.random.fold_in(key, 11), WIN // 2).astype(jnp.int32)
    return jnp.stack([shuffle, WIN - 1 - shuffle], axis=1).reshape(WIN).astype(jnp.int32)


def draw_wave_of_slot(key, part):
    return paired_waves(key)


def draw_first_tile(key, part):
    waves_here = paired_waves(key)
    wavenumber = waves_here * NDEG // WIN
    extra_tile = jax.random.randint(jax.random.fold_in(key, 12), (WIN,), 0, 2).astype(jnp.int32)
    tiles_here = wavenumber * TILES // NDEG + extra_tile * (wavenumber > 0).astype(jnp.int32)
    tiles_here = jnp.minimum(tiles_here, TILES - 1)
    tiles_here = jnp.where(waves_here == WIN - 1, TILES - 1, tiles_here)
    return tiles_here.astype(jnp.int32)


def level_of(rng, dims, split, smallest, high):
    loudness = 1.0
    for position, blocks in split:
        steps = jax.random.uniform(jax.random.fold_in(jax.random.fold_in(rng, 6), position), (blocks,), jnp.float32, smallest / len(split), high / len(split))
        loudness = loudness * jnp.repeat(jnp.exp(steps), dims[position] // blocks).reshape((-1,) + (1,) * (len(dims) - 1 - position))
    return loudness


def scatter_about(rng, dims, scale, reach, split=(), dtype=jnp.bfloat16):
    array = scale * jax.random.normal(rng, dims, jnp.float32)
    if split:
        array = array * level_of(rng, dims, split, -0.22, 0.18)
    return jnp.clip(array, -reach, reach).astype(dtype)


def setup_inputs(seed: int = 0) -> dict:
    key_of = jax.random.split(jax.random.key(seed), 7)
    return {
        "grid_data": scatter_about(key_of[0], (NLAT, WIN, COLS), 1.0, 6.0, ((0, 8), (2, 4)), jnp.float32),
        "legendre": scatter_about(key_of[1], (WIN, HALF, NDEG), NLAT ** -0.5, 0.125, ((0, 8),), jnp.float32),
        "gauss_weights": jnp.clip(jnp.exp(jax.random.uniform(key_of[2], (HALF,), jnp.float32, math.log(0.4), math.log(2.0))), 0.4, 2.0),
        "wave_of_slot": draw_wave_of_slot(jax.random.fold_in(key_of[6], 71), 0),
        "first_tile": draw_first_tile(jax.random.fold_in(key_of[6], 71), 0),
        "coupling": scatter_about(key_of[5], (LEVELS, LEVELS), LEVELS ** -0.5, 0.75, ((1, 4),), jnp.float32),
    }


def reference(grid_data, legendre, gauss_weights, wave_of_slot, first_tile, coupling):
    lat_index = jnp.arange(HALF)
    degree_index = jnp.arange(NDEG)
    implicit_factor = (degree_index * (degree_index + 1)).astype(jnp.float32) / float(NDEG * (NDEG - 1))
    quadrature = jnp.concatenate([gauss_weights, gauss_weights[::-1]])

    def one_slot(packed):
        legendre_slot, wave_slot, first_slot = packed
        wavenumber = (wave_slot * NDEG) // WIN
        kept_mask = ((lat_index // TILE) >= first_slot)[:, None] & (degree_index >= wavenumber)[None, :]
        northern = jnp.where(kept_mask, legendre_slot, jnp.zeros_like(legendre_slot))
        parity = jnp.where((degree_index + wavenumber) % 2 == 0, 1.0, -1.0).astype(jnp.float32)
        full_table = jnp.concatenate([northern, (northern * parity[None, :])[::-1]], axis=0)
        column_data = lax.dynamic_index_in_dim(grid_data, wave_slot, 1, keepdims=False)
        spectral = jnp.dot(full_table.T, quadrature[:, None] * column_data,
                           precision=lax.Precision.HIGHEST, preferred_element_type=jnp.float32)
        spectral_split = spectral.reshape(NDEG, LEVELS, 6)
        divergence = spectral_split[:, :, 2:4]
        coupled = jnp.einsum('ab,nbk->nak', coupling, divergence, precision=lax.Precision.HIGHEST)
        updated = divergence - implicit_factor[:, None, None] * coupled
        spectral_split = jnp.concatenate([spectral_split[:, :, :2], updated, spectral_split[:, :, 4:]], axis=2)
        return jnp.dot(full_table, spectral_split.reshape(NDEG, COLS),
                       precision=lax.Precision.HIGHEST, preferred_element_type=jnp.float32)

    per_slot = lax.map(one_slot, (legendre, wave_of_slot, first_tile))
    placed = jnp.zeros_like(per_slot).at[wave_of_slot].set(per_slot)
    return jnp.transpose(placed, (1, 0, 2))
```

```python
import functools

import jax
import jax.numpy as jnp
from jax import lax
from jax.experimental import pallas as pl
from jax.experimental.pallas import tpu as pltpu
from jax.sharding import PartitionSpec as P

TILE = 128
FIELDS = 6
PAIR = 2
FIRST = 2
MESH = pl.DeviceIdType.MESH
NN = (((1,), (0,)), ((), ()))
NT = (((1,), (1,)), ((), ()))
VMEM_BYTES = 64 * 1024 * 1000


def mm(a, b, dims=NN):
    return lax.dot_general(a, b, dims, preferred_element_type=jnp.float32)


def split(v):
    high = v.astype(jnp.bfloat16)
    return high, (v - high.astype(jnp.float32)).astype(jnp.bfloat16)


def mm3(a_high, a_low, b_high, b_low, dims=NN):
    return mm(a_high, b_high, dims) + (mm(a_low, b_high, dims) + mm(a_high, b_low, dims))


def iota(shape, axis):
    return lax.broadcasted_iota(jnp.int32, shape, axis)


def pack_kernel(wave_ref, x_ref, out_ref):
    waves = wave_ref.shape[0]
    lats = out_ref.shape[2]
    wave = wave_ref[pl.program_id(0)]
    out_ref[0] = x_ref[pl.ds(wave, lats, stride=waves), :].T


def pack(wave_of_slot, grid_data):
    lats, waves, cols = grid_data.shape
    return pl.pallas_call(
        pack_kernel,
        grid_spec=pltpu.PrefetchScalarGridSpec(
            num_scalar_prefetch=1,
            grid=(waves,),
            in_specs=[pl.BlockSpec((lats * waves, cols), lambda s, w: (0, 0))],
            out_specs=pl.BlockSpec((1, cols, lats), lambda s, w: (s, 0, 0)),
        ),
        out_shape=jax.ShapeDtypeStruct((waves, cols, lats), jnp.float32),
        compiler_params=pltpu.CompilerParams(vmem_limit_bytes=VMEM_BYTES),
        name="pack",
    )(wave_of_slot, grid_data.reshape(lats * waves, cols))


def unpack_kernel(wave_ref, y_ref, out_ref):
    waves = wave_ref.shape[0]
    lats = y_ref.shape[2]
    wave = wave_ref[pl.program_id(0)]
    out_ref[pl.ds(wave, lats, stride=waves), :] = y_ref[0].T


def unpack(wave_of_slot, packed):
    waves, cols, lats = packed.shape
    out = pl.pallas_call(
        unpack_kernel,
        grid_spec=pltpu.PrefetchScalarGridSpec(
            num_scalar_prefetch=1,
            grid=(waves,),
            in_specs=[pl.BlockSpec((1, cols, lats), lambda s, w: (s, 0, 0))],
            out_specs=pl.BlockSpec((lats * waves, cols), lambda s, w: (0, 0)),
        ),
        out_shape=jax.ShapeDtypeStruct((lats * waves, cols), jnp.float32),
        compiler_params=pltpu.CompilerParams(vmem_limit_bytes=VMEM_BYTES),
        name="unpack",
    )(wave_of_slot, packed)
    return out.reshape(lats, waves, cols)


def spectral_kernel(
    W, NL,
    wave_ref, tile_ref, gauss_ref, coupling_ref, packed_ref, tables_ref, out_ref,
    tab, recv, osend, lev_send, lev_recv, x_high, x_low, spec, r_high, r_low, k_high, k_low,
    tab_sem, own_sem, in_send, in_recv, lev_ssem, lev_rsem, out_own, out_send, out_recv,
):
    SL, H, N = tab.shape
    C, LAT = recv.shape[2], recv.shape[3]
    waves = wave_ref.shape[0]
    LP = C // FIELDS
    half = W // 2
    TW = max(256, LAT)
    BPT = TW // LAT
    nt = H // TW
    NW = 256
    me = lax.axis_index("wave")
    ml = lax.axis_index("lev")
    order = sorted(range(1, W), key=lambda d: (abs(d - half), d))
    lev_order = sorted(range(1, NL), key=lambda d: (abs(d - NL // 2), d))

    barrier = pltpu.get_barrier_semaphore()
    for d in range(1, W):
        pl.semaphore_signal(barrier, inc=1, device_id=(lax.rem(me + d, W), ml), device_id_type=MESH)
    for d in range(1, NL):
        pl.semaphore_signal(barrier, inc=1, device_id=(me, lax.rem(ml + d, NL)), device_id_type=MESH)
    pl.semaphore_wait(barrier, W - 1 + NL - 1)

    def in_copy(s, d):
        dst = lax.rem(me + d, W)
        return pltpu.make_async_remote_copy(
            src_ref=packed_ref.at[dst * SL + s], dst_ref=recv.at[s, me],
            send_sem=in_send.at[s, d], recv_sem=in_recv.at[s, d],
            device_id=(dst, ml), device_id_type=MESH)

    def in_arrival(s, d):
        src = lax.rem(me + W - d, W)
        return pltpu.make_async_remote_copy(
            src_ref=packed_ref.at[me * SL + s], dst_ref=recv.at[s, src],
            send_sem=in_send.at[s, d], recv_sem=in_recv.at[s, d],
            device_id=(src, ml), device_id_type=MESH)

    def out_copy(s, d):
        dst = lax.rem(me + d, W)
        return pltpu.make_async_remote_copy(
            src_ref=osend.at[s, dst], dst_ref=out_ref.at[me * SL + s],
            send_sem=out_send.at[s, d], recv_sem=out_recv.at[s, d],
            device_id=(dst, ml), device_id_type=MESH)

    def out_arrival(s, d):
        src = lax.rem(me + W - d, W)
        return pltpu.make_async_remote_copy(
            src_ref=osend.at[s, src], dst_ref=out_ref.at[src * SL + s],
            send_sem=out_send.at[s, d], recv_sem=out_recv.at[s, d],
            device_id=(src, ml), device_id_type=MESH)

    def lev_copy(s, d):
        dst = lax.rem(ml + d, NL)
        return pltpu.make_async_remote_copy(
            src_ref=lev_send.at[s, dst], dst_ref=lev_recv.at[s, ml],
            send_sem=lev_ssem.at[s, d], recv_sem=lev_rsem.at[s, d],
            device_id=(me, dst), device_id_type=MESH)

    def lev_arrival(s, d):
        src = lax.rem(ml + NL - d, NL)
        return pltpu.make_async_remote_copy(
            src_ref=lev_send.at[s, src], dst_ref=lev_recv.at[s, src],
            send_sem=lev_ssem.at[s, d], recv_sem=lev_rsem.at[s, d],
            device_id=(me, src), device_id_type=MESH)

    def own_in(s):
        return pltpu.make_async_copy(packed_ref.at[me * SL + s], recv.at[s, me], own_sem.at[s])

    def own_out(s):
        return pltpu.make_async_copy(osend.at[s, me], out_ref.at[me * SL + s], out_own.at[s])

    def table_in(s):
        return pltpu.make_async_copy(tables_ref.at[s], tab.at[s], tab_sem.at[s])

    @pl.loop(0, SL)
    def _(s):
        for d in order:
            in_copy(s, d).start()
        own_in(s).start()
        table_in(s).start()

    rows = PAIR * LP * NL
    levels = LP * NL
    up = (iota((rows, levels), 0) // PAIR == iota((rows, levels), 1)).astype(jnp.float32)
    down = (iota((LP, C), 0) == iota((LP, C), 1) // FIELDS).astype(jnp.float32)
    wide = jnp.dot(
        jnp.dot(up, coupling_ref[...], precision=lax.Precision.HIGHEST), down,
        precision=lax.Precision.HIGHEST)
    kept = iota((rows, C), 1) % FIELDS == iota((rows, C), 0) % PAIR + FIRST
    k_high[...], k_low[...] = split(jnp.where(kept, wide, 0.0))
    er, ec = iota((C, rows), 0), iota((C, rows), 1) % (PAIR * LP)
    expand = ((er // FIELDS == ec // PAIR) & (er % FIELDS == ec % PAIR + FIRST)).astype(jnp.float32)
    expand = expand.astype(jnp.bfloat16)
    flip = (iota((TW, TW), 0) + iota((TW, TW), 1) == TW - 1).astype(jnp.float32).astype(jnp.bfloat16)

    def flipped(v):
        high, low = split(v)
        return mm(high, flip) + mm(low, flip)

    @pl.loop(0, SL)
    def _(s):
        wave = wave_ref[me * SL + s]
        first = tile_ref[s] * TILE
        m = (wave * N) // waves
        for d in order:
            in_arrival(s, d).wait_recv()
        own_in(s).wait()
        table_in(s).wait()

        for t in range(nt):
            north = jnp.concatenate([recv[s, t * BPT + b] for b in range(BPT)], axis=1)
            south = jnp.concatenate([recv[s, half + t * BPT + b] for b in range(BPT)], axis=1)
            south = flipped(south)
            for v, at, row in ((north, t, 0), (south, nt - 1 - t, C)):
                lanes = pl.ds(at * TW, TW)
                used = iota((1, TW), 1) + at * TW >= first
                scaled = v * jnp.where(used, gauss_ref[:, lanes], 0.0)
                high, low = split(scaled)
                x_high[pl.ds(row, C), lanes] = high
                x_low[pl.ds(row, C), lanes] = low

        @pl.loop(0, N // NW)
        def _(j):
            lanes = pl.ds(pl.multiple_of(j * NW, NW), NW)
            t_high, t_low = split(tab[s, :, lanes])
            f = mm3(x_high[...], x_low[...], t_high, t_low)
            degree = iota((1, NW), 1) + j * NW
            used = degree >= m
            sign = jnp.where((degree + m) % 2 == 0, 1.0, -1.0)
            spectral = jnp.where(used, f[:C] + sign * f[C:], 0.0)
            spec[:, lanes] = spectral
            s_high, s_low = split(spectral)
            part = mm3(k_high[...], k_low[...], s_high, s_low)
            for l in range(NL):
                lev_send[s, l, :, lanes] = part[l * PAIR * LP:(l + 1) * PAIR * LP]

        lev_recv[s, ml] = lev_send[s, ml]
        for d in lev_order:
            lev_copy(s, d).start()
        for d in lev_order:
            lev_arrival(s, d).wait_recv()

        @pl.loop(0, N // NW)
        def _(j):
            lanes = pl.ds(pl.multiple_of(j * NW, NW), NW)
            degree = iota((1, NW), 1) + j * NW
            sign = jnp.where((degree + m) % 2 == 0, 1.0, -1.0)
            factor = (degree * (degree + 1)).astype(jnp.float32) / float(N * (N - 1))
            p_high, p_low = split(jnp.concatenate([lev_recv[s, l, :, lanes] for l in range(NL)], axis=0))
            coupled = mm(expand, p_high) + mm(expand, p_low)
            updated = spec[:, lanes] - factor * coupled
            u_high, u_low = split(updated)
            r_high[pl.ds(0, C), lanes] = u_high
            r_low[pl.ds(0, C), lanes] = u_low
            w_high, w_low = split(sign * updated)
            r_high[pl.ds(C, C), lanes] = w_high
            r_low[pl.ds(C, C), lanes] = w_low

        @pl.loop(0, nt)
        def _(i):
            rows_here = pl.ds(pl.multiple_of(i * TW, TW), TW)
            t_high, t_low = split(tab[s, rows_here, :])
            o = mm3(r_high[...], r_low[...], t_high, t_low, NT)
            used = iota((1, TW), 1) + i * TW >= first
            o = jnp.where(used, o, 0.0)
            north = o[:C]
            south = flipped(o[C:])
            for b in range(BPT):
                cut = slice(b * LAT, (b + 1) * LAT)
                osend[s, i * BPT + b] = north[:, cut]
                osend[s, half + (nt - 1 - i) * BPT + b] = south[:, cut]

        for d in order:
            out_copy(s, d).start()
        own_out(s).start()

    @pl.loop(0, SL)
    def _(s):
        own_out(s).wait()
        for d in order:
            in_copy(s, d).wait_send()
            out_copy(s, d).wait_send()
            out_arrival(s, d).wait_recv()
        for d in lev_order:
            lev_copy(s, d).wait_send()


def transform(W, NL, packed, legendre, gauss_weights, wave_of_slot, first_tile, coupling):
    waves, C, LAT = packed.shape
    SL, H, N = legendre.shape
    rows = PAIR * (C // FIELDS)
    f32, bf16, dma = jnp.float32, jnp.bfloat16, pltpu.SemaphoreType.DMA
    vmem = pl.BlockSpec(memory_space=pltpu.VMEM)
    smem = pl.BlockSpec(memory_space=pltpu.SMEM)
    hbm = pl.BlockSpec(memory_space=pl.ANY)
    return pl.pallas_call(
        functools.partial(spectral_kernel, W, NL),
        out_shape=jax.ShapeDtypeStruct((waves, C, LAT), f32),
        in_specs=[smem, smem, vmem, vmem, hbm, hbm],
        out_specs=hbm,
        scratch_shapes=[
            pltpu.VMEM((SL, H, N), f32),
            pltpu.VMEM((SL, W, C, LAT), f32),
            pltpu.VMEM((SL, W, C, LAT), f32),
            pltpu.VMEM((SL, NL, rows, N), f32),
            pltpu.VMEM((SL, NL, rows, N), f32),
            pltpu.VMEM((2 * C, H), bf16),
            pltpu.VMEM((2 * C, H), bf16),
            pltpu.VMEM((C, N), f32),
            pltpu.VMEM((2 * C, N), bf16),
            pltpu.VMEM((2 * C, N), bf16),
            pltpu.VMEM((rows * NL, C), bf16),
            pltpu.VMEM((rows * NL, C), bf16),
            dma((SL,)), dma((SL,)),
            dma((SL, W)), dma((SL, W)),
            dma((SL, NL)), dma((SL, NL)),
            dma((SL,)), dma((SL, W)), dma((SL, W)),
        ],
        compiler_params=pltpu.CompilerParams(
            collective_id=0, has_side_effects=True, vmem_limit_bytes=VMEM_BYTES),
        name="spectral",
    )(wave_of_slot, first_tile, gauss_weights[None, :], coupling, packed, legendre)


def solution(mesh):
    W, NL = mesh.shape["wave"], mesh.shape["lev"]

    def shards(grid_data, legendre, gauss_weights, wave_of_slot, first_tile, coupling):
        packed = pack(wave_of_slot, grid_data)
        back = transform(W, NL, packed, legendre, gauss_weights, wave_of_slot, first_tile, coupling)
        return unpack(wave_of_slot, back)

    placed = (P("wave", None, "lev"), P("wave", None, None), P(), P(), P("wave"), P(None, "lev"))
    return jax.shard_map(
        shards, mesh=mesh, in_specs=placed, out_specs=P("wave", None, "lev"), check_vma=False
    )
```

```python
import functools

import jax
import jax.numpy as jnp
from jax import lax
from jax.experimental import pallas as pl
from jax.experimental.pallas import tpu as pltpu
from jax.sharding import PartitionSpec as P

TILE = 128
FIELDS = 6
PAIR = 2
FIRST = 2
MESH = pl.DeviceIdType.MESH
NN = (((1,), (0,)), ((), ()))
NT = (((1,), (1,)), ((), ()))
VMEM_BYTES = 64 * 1024 * 1000


def mm(a, b, dims=NN):
    return lax.dot_general(a, b, dims, preferred_element_type=jnp.float32)


def split(v):
    high = v.astype(jnp.bfloat16)
    return high, (v - high.astype(jnp.float32)).astype(jnp.bfloat16)


def mm3(a_high, a_low, b_high, b_low, dims=NN):
    return mm(a_high, b_high, dims) + (mm(a_low, b_high, dims) + mm(a_high, b_low, dims))


def iota(shape, axis):
    return lax.broadcasted_iota(jnp.int32, shape, axis)


def unpack_kernel(wave_ref, y_ref, out_ref, held, in_sem, out_sem):
    waves = wave_ref.shape[0]

    def fetch(s):
        return pltpu.make_async_copy(y_ref.at[s], held.at[s], in_sem.at[s])

    def put(s):
        return pltpu.make_async_copy(held.at[s], out_ref.at[wave_ref[s]], out_sem.at[s])

    @pl.loop(0, waves)
    def _(s):
        fetch(s).start()

    @pl.loop(0, waves)
    def _(s):
        fetch(s).wait()
        put(s).start()

    @pl.loop(0, waves)
    def _(s):
        put(s).wait()


def unpack(wave_of_slot, packed):
    waves = packed.shape[0]
    return pl.pallas_call(
        unpack_kernel,
        out_shape=jax.ShapeDtypeStruct(packed.shape, jnp.float32),
        in_specs=[pl.BlockSpec(memory_space=pltpu.SMEM), pl.BlockSpec(memory_space=pl.ANY)],
        out_specs=pl.BlockSpec(memory_space=pl.ANY),
        scratch_shapes=[
            pltpu.VMEM(packed.shape, jnp.float32),
            pltpu.SemaphoreType.DMA((waves,)),
            pltpu.SemaphoreType.DMA((waves,)),
        ],
        compiler_params=pltpu.CompilerParams(vmem_limit_bytes=VMEM_BYTES),
        name="unpack",
    )(wave_of_slot, packed)


def spectral_kernel(
    W, NL,
    wave_ref, tile_ref, gauss_ref, coupling_ref, grid_ref, tables_ref, out_ref,
    held, stage, tab, recv, osend, lev_send, lev_recv, x_high, x_low, spec, r_high, r_low, k_high, k_low,
    held_sem, tab_sem, own_sem, in_send, in_recv, lev_ssem, lev_rsem, out_own, out_send, out_recv,
):
    SL, H, N = tab.shape
    C, LAT = recv.shape[2], recv.shape[3]
    waves = wave_ref.shape[0]
    LP = C // FIELDS
    half = W // 2
    TW = max(256, LAT)
    BPT = TW // LAT
    nt = H // TW
    NW = 256
    me = lax.axis_index("wave")
    ml = lax.axis_index("lev")
    order = sorted(range(1, W), key=lambda d: (abs(d - half), d))
    lev_order = sorted(range(1, NL), key=lambda d: (abs(d - NL // 2), d))

    held_copy = pltpu.make_async_copy(grid_ref, held, held_sem)
    held_copy.start()
    barrier = pltpu.get_barrier_semaphore()
    for d in range(1, W):
        pl.semaphore_signal(barrier, inc=1, device_id=(lax.rem(me + d, W), ml), device_id_type=MESH)
    for d in range(1, NL):
        pl.semaphore_signal(barrier, inc=1, device_id=(me, lax.rem(ml + d, NL)), device_id_type=MESH)
    pl.semaphore_wait(barrier, W - 1 + NL - 1)

    def in_copy(s, d):
        dst = lax.rem(me + d, W)
        return pltpu.make_async_remote_copy(
            src_ref=stage.at[dst * SL + s], dst_ref=recv.at[s, me],
            send_sem=in_send.at[s, d], recv_sem=in_recv.at[s, d],
            device_id=(dst, ml), device_id_type=MESH)

    def in_arrival(s, d):
        src = lax.rem(me + W - d, W)
        return pltpu.make_async_remote_copy(
            src_ref=stage.at[me * SL + s], dst_ref=recv.at[s, src],
            send_sem=in_send.at[s, d], recv_sem=in_recv.at[s, d],
            device_id=(src, ml), device_id_type=MESH)

    def out_copy(s, d):
        dst = lax.rem(me + d, W)
        return pltpu.make_async_remote_copy(
            src_ref=osend.at[s, dst], dst_ref=out_ref.at[me * SL + s],
            send_sem=out_send.at[s, d], recv_sem=out_recv.at[s, d],
            device_id=(dst, ml), device_id_type=MESH)

    def out_arrival(s, d):
        src = lax.rem(me + W - d, W)
        return pltpu.make_async_remote_copy(
            src_ref=osend.at[s, src], dst_ref=out_ref.at[src * SL + s],
            send_sem=out_send.at[s, d], recv_sem=out_recv.at[s, d],
            device_id=(src, ml), device_id_type=MESH)

    def lev_copy(s, d):
        dst = lax.rem(ml + d, NL)
        return pltpu.make_async_remote_copy(
            src_ref=lev_send.at[s, dst], dst_ref=lev_recv.at[s, ml],
            send_sem=lev_ssem.at[s, d], recv_sem=lev_rsem.at[s, d],
            device_id=(me, dst), device_id_type=MESH)

    def lev_arrival(s, d):
        src = lax.rem(ml + NL - d, NL)
        return pltpu.make_async_remote_copy(
            src_ref=lev_send.at[s, src], dst_ref=lev_recv.at[s, src],
            send_sem=lev_ssem.at[s, d], recv_sem=lev_rsem.at[s, d],
            device_id=(me, src), device_id_type=MESH)

    def own_in(s):
        return pltpu.make_async_copy(stage.at[me * SL + s], recv.at[s, me], own_sem.at[s])

    def own_out(s):
        return pltpu.make_async_copy(osend.at[s, me], out_ref.at[me * SL + s], out_own.at[s])

    def table_in(s):
        return pltpu.make_async_copy(tables_ref.at[s], tab.at[s], tab_sem.at[s])

    held_copy.wait()

    @pl.loop(0, waves)
    def _(s):
        stage[s] = held[wave_ref[s]]

    @pl.loop(0, SL)
    def _(s):
        for d in order:
            in_copy(s, d).start()
        own_in(s).start()
        table_in(s).start()

    rows = PAIR * LP * NL
    levels = LP * NL
    up = (iota((rows, levels), 0) // PAIR == iota((rows, levels), 1)).astype(jnp.float32)
    down = (iota((LP, C), 0) == iota((LP, C), 1) // FIELDS).astype(jnp.float32)
    wide = jnp.dot(
        lax.dot_general(up, coupling_ref[...], NT, precision=lax.Precision.HIGHEST), down,
        precision=lax.Precision.HIGHEST)
    kept = iota((rows, C), 1) % FIELDS == iota((rows, C), 0) % PAIR + FIRST
    k_high[...], k_low[...] = split(jnp.where(kept, wide, 0.0))
    er, ec = iota((C, rows), 0), iota((C, rows), 1) % (PAIR * LP)
    expand = ((er // FIELDS == ec // PAIR) & (er % FIELDS == ec % PAIR + FIRST)).astype(jnp.float32)
    expand = expand.astype(jnp.bfloat16)
    flip = (iota((TW, TW), 0) + iota((TW, TW), 1) == TW - 1).astype(jnp.float32).astype(jnp.bfloat16)

    def flipped(v):
        high, low = split(v)
        return mm(high, flip) + mm(low, flip)

    @pl.loop(0, SL)
    def _(s):
        wave = wave_ref[me * SL + s]
        first = tile_ref[s] * TILE
        m = (wave * N) // waves
        for d in order:
            in_arrival(s, d).wait_recv()
        own_in(s).wait()
        table_in(s).wait()

        for t in range(nt):
            north = jnp.concatenate([recv[s, t * BPT + b] for b in range(BPT)], axis=1)
            south = jnp.concatenate([recv[s, half + t * BPT + b] for b in range(BPT)], axis=1)
            south = flipped(south)
            for v, at, row in ((north, t, 0), (south, nt - 1 - t, C)):
                lanes = pl.ds(at * TW, TW)
                used = iota((1, TW), 1) + at * TW >= first
                scaled = v * jnp.where(used, gauss_ref[:, lanes], 0.0)
                high, low = split(scaled)
                x_high[pl.ds(row, C), lanes] = high
                x_low[pl.ds(row, C), lanes] = low

        @pl.loop(0, N // NW)
        def _(j):
            lanes = pl.ds(pl.multiple_of(j * NW, NW), NW)
            t_high, t_low = split(tab[s, :, lanes])
            f = mm3(x_high[...], x_low[...], t_high, t_low)
            degree = iota((1, NW), 1) + j * NW
            used = degree >= m
            sign = jnp.where((degree + m) % 2 == 0, 1.0, -1.0)
            spectral = jnp.where(used, f[:C] + sign * f[C:], 0.0)
            spec[:, lanes] = spectral
            s_high, s_low = split(spectral)
            part = mm3(k_high[...], k_low[...], s_high, s_low)
            for l in range(NL):
                lev_send[s, l, :, lanes] = part[l * PAIR * LP:(l + 1) * PAIR * LP]

        lev_recv[s, ml] = lev_send[s, ml]
        for d in lev_order:
            lev_copy(s, d).start()
        for d in lev_order:
            lev_arrival(s, d).wait_recv()

        @pl.loop(0, N // NW)
        def _(j):
            lanes = pl.ds(pl.multiple_of(j * NW, NW), NW)
            degree = iota((1, NW), 1) + j * NW
            sign = jnp.where((degree + m) % 2 == 0, 1.0, -1.0)
            factor = (degree * (degree + 1)).astype(jnp.float32) / float(N * (N - 1))
            p_high, p_low = split(jnp.concatenate([lev_recv[s, l, :, lanes] for l in range(NL)], axis=0))
            coupled = mm(expand, p_high) + mm(expand, p_low)
            updated = spec[:, lanes] - factor * coupled
            u_high, u_low = split(updated)
            r_high[pl.ds(0, C), lanes] = u_high
            r_low[pl.ds(0, C), lanes] = u_low
            w_high, w_low = split(sign * updated)
            r_high[pl.ds(C, C), lanes] = w_high
            r_low[pl.ds(C, C), lanes] = w_low

        @pl.loop(0, nt)
        def _(i):
            rows_here = pl.ds(pl.multiple_of(i * TW, TW), TW)
            t_high, t_low = split(tab[s, rows_here, :])
            o = mm3(r_high[...], r_low[...], t_high, t_low, NT)
            used = iota((1, TW), 1) + i * TW >= first
            o = jnp.where(used, o, 0.0)
            north = o[:C]
            south = flipped(o[C:])
            for b in range(BPT):
                cut = slice(b * LAT, (b + 1) * LAT)
                osend[s, i * BPT + b] = north[:, cut]
                osend[s, half + (nt - 1 - i) * BPT + b] = south[:, cut]

        for d in order:
            out_copy(s, d).start()
        own_out(s).start()

    @pl.loop(0, SL)
    def _(s):
        own_out(s).wait()
        for d in order:
            in_copy(s, d).wait_send()
            out_copy(s, d).wait_send()
            out_arrival(s, d).wait_recv()
        for d in lev_order:
            lev_copy(s, d).wait_send()


def transform(W, NL, grid, legendre, gauss_weights, wave_of_slot, first_tile, coupling):
    waves, C, LAT = grid.shape
    SL, H, N = legendre.shape
    rows = PAIR * (C // FIELDS)
    f32, bf16, dma = jnp.float32, jnp.bfloat16, pltpu.SemaphoreType.DMA
    vmem = pl.BlockSpec(memory_space=pltpu.VMEM)
    smem = pl.BlockSpec(memory_space=pltpu.SMEM)
    hbm = pl.BlockSpec(memory_space=pl.ANY)
    return pl.pallas_call(
        functools.partial(spectral_kernel, W, NL),
        out_shape=jax.ShapeDtypeStruct((waves, C, LAT), f32),
        in_specs=[smem, smem, vmem, vmem, hbm, hbm],
        out_specs=hbm,
        scratch_shapes=[
            pltpu.VMEM((waves, C, LAT), f32),
            pltpu.VMEM((waves, C, LAT), f32),
            pltpu.VMEM((SL, H, N), f32),
            pltpu.VMEM((SL, W, C, LAT), f32),
            pltpu.VMEM((SL, W, C, LAT), f32),
            pltpu.VMEM((SL, NL, rows, N), f32),
            pltpu.VMEM((SL, NL, rows, N), f32),
            pltpu.VMEM((2 * C, H), bf16),
            pltpu.VMEM((2 * C, H), bf16),
            pltpu.VMEM((C, N), f32),
            pltpu.VMEM((2 * C, N), bf16),
            pltpu.VMEM((2 * C, N), bf16),
            pltpu.VMEM((rows * NL, C), bf16),
            pltpu.VMEM((rows * NL, C), bf16),
            dma, dma((SL,)), dma((SL,)),
            dma((SL, W)), dma((SL, W)),
            dma((SL, NL)), dma((SL, NL)),
            dma((SL,)), dma((SL, W)), dma((SL, W)),
        ],
        compiler_params=pltpu.CompilerParams(
            collective_id=0, has_side_effects=True, vmem_limit_bytes=VMEM_BYTES),
        name="spectral",
    )(wave_of_slot, first_tile, gauss_weights[None, :], coupling.T, grid, legendre)


def solution(mesh):
    W, NL = mesh.shape["wave"], mesh.shape["lev"]

    def shards(grid_data, legendre, gauss_weights, wave_of_slot, first_tile, coupling):
        grid = jnp.transpose(grid_data, (1, 2, 0))
        back = transform(W, NL, grid, legendre, gauss_weights, wave_of_slot, first_tile, coupling)
        return jnp.transpose(unpack(wave_of_slot, back), (2, 0, 1))

    placed = (P("wave", None, "lev"), P("wave", None, None), P(), P(), P("wave"), P(None, "lev"))
    return jax.shard_map(
        shards, mesh=mesh, in_specs=placed, out_specs=P("wave", None, "lev"), check_vma=False
    )
```

```python
import functools

import jax
import jax.numpy as jnp
from jax import lax
from jax.experimental import pallas as pl
from jax.experimental.pallas import tpu as pltpu
from jax.sharding import PartitionSpec as P

TILE = 128
FIELDS = 6
PAIR = 2
FIRST = 2
MESH = pl.DeviceIdType.MESH
NN = (((1,), (0,)), ((), ()))
NT = (((1,), (1,)), ((), ()))
VMEM_BYTES = 64 * 1024 * 1000


def mm(a, b, dims=NN):
    return lax.dot_general(a, b, dims, preferred_element_type=jnp.float32)


def split(v):
    high = v.astype(jnp.bfloat16)
    return high, (v - high.astype(jnp.float32)).astype(jnp.bfloat16)


def mm3(a_high, a_low, b_high, b_low, dims=NN):
    return mm(a_high, b_high, dims) + (mm(a_low, b_high, dims) + mm(a_high, b_low, dims))


def iota(shape, axis):
    return lax.broadcasted_iota(jnp.int32, shape, axis)


def polar(w, W):
    return (w < W // 4) | (w >= W - W // 4)


def unpack_kernel(W, compact, wave_ref, y_ref, out_ref, held, zero, in_sem, out_sem):
    waves = wave_ref.shape[0]
    halved = polar(lax.axis_index("wave"), W) if compact else False

    def source(s):
        return jnp.where(halved, s - s % 2, s) if compact else s

    def fetch(s):
        return pltpu.make_async_copy(y_ref.at[source(s)], held.at[s], in_sem.at[s])

    def put(s, src):
        return pltpu.make_async_copy(src, out_ref.at[wave_ref[s]], out_sem.at[s])

    @pl.loop(0, waves)
    def _(s):
        fetch(s).start()

    if compact:
        zero[...] = jnp.zeros_like(zero)

    @pl.loop(0, waves)
    def _(s):
        fetch(s).wait()
        if compact:
            empty = halved & (wave_ref[s] > wave_ref[s + 1 - 2 * (s % 2)])

            @pl.when(empty)
            def _():
                put(s, zero).start()

            @pl.when(jnp.logical_not(empty))
            def _():
                put(s, held.at[s]).start()
        else:
            put(s, held.at[s]).start()

    @pl.loop(0, waves)
    def _(s):
        put(s, held.at[s]).wait()


def unpack(W, compact, wave_of_slot, packed):
    waves = packed.shape[0]
    return pl.pallas_call(
        functools.partial(unpack_kernel, W, compact),
        out_shape=jax.ShapeDtypeStruct(packed.shape, jnp.float32),
        in_specs=[pl.BlockSpec(memory_space=pltpu.SMEM), pl.BlockSpec(memory_space=pl.ANY)],
        out_specs=pl.BlockSpec(memory_space=pl.ANY),
        scratch_shapes=[
            pltpu.VMEM(packed.shape, jnp.float32),
            pltpu.VMEM(packed.shape[1:], jnp.float32),
            pltpu.SemaphoreType.DMA((waves,)),
            pltpu.SemaphoreType.DMA((waves,)),
        ],
        compiler_params=pltpu.CompilerParams(vmem_limit_bytes=VMEM_BYTES),
        name="unpack_half" if compact else "unpack",
    )(wave_of_slot, packed)


def spectral_kernel(
    W, NL, compact,
    wave_ref, tile_ref, gauss_ref, coupling_ref, grid_ref, tables_ref, out_ref, flag_ref,
    held, stage, tab, recv, osend, lev_send, lev_recv, x_high, x_low, spec, r_high, r_low, k_high, k_low,
    held_sem, tab_sem, own_sem, in_send, in_recv, lev_ssem, lev_rsem, out_own, out_send, out_recv,
    flags, flag_send, flag_recv,
):
    SL, H, N = tab.shape
    C, LAT = recv.shape[2], recv.shape[3]
    waves = wave_ref.shape[0]
    LP = C // FIELDS
    half = W // 2
    TW = max(256, LAT)
    BPT = TW // LAT
    nt = H // TW
    NW = 256
    me = lax.axis_index("wave")
    ml = lax.axis_index("lev")
    order = sorted(range(1, W), key=lambda d: (abs(d - half), d))
    lev_order = sorted(range(1, NL), key=lambda d: (abs(d - NL // 2), d))

    held_copy = pltpu.make_async_copy(grid_ref, held, held_sem)
    held_copy.start()
    def halved(w):
        return polar(w, W) if compact else False

    def full_turn(w, s, parity):
        return jnp.logical_not(halved(w)) | (s % 2 == parity) if compact else s >= 0

    def block(w, s):
        return jnp.where(halved(w), s - s % 2, s) if compact else s

    barrier = pltpu.get_barrier_semaphore()
    for d in range(1, W):
        pl.semaphore_signal(barrier, inc=1, device_id=(lax.rem(me + d, W), ml), device_id_type=MESH)
    for d in range(1, NL):
        pl.semaphore_signal(barrier, inc=1, device_id=(me, lax.rem(ml + d, NL)), device_id_type=MESH)
    pl.semaphore_wait(barrier, W - 1 + NL - 1)

    def in_copy(s, d):
        dst = lax.rem(me + d, W)
        return pltpu.make_async_remote_copy(
            src_ref=stage.at[dst * SL + s], dst_ref=recv.at[s, me],
            send_sem=in_send.at[s, d], recv_sem=in_recv.at[s, d],
            device_id=(dst, ml), device_id_type=MESH)

    def in_arrival(s, d):
        src = lax.rem(me + W - d, W)
        return pltpu.make_async_remote_copy(
            src_ref=stage.at[me * SL + s], dst_ref=recv.at[s, src],
            send_sem=in_send.at[s, d], recv_sem=in_recv.at[s, d],
            device_id=(src, ml), device_id_type=MESH)

    def out_copy(s, d):
        dst = lax.rem(me + d, W)
        return pltpu.make_async_remote_copy(
            src_ref=osend.at[block(dst, s), dst], dst_ref=out_ref.at[me * SL + block(dst, s)],
            send_sem=out_send.at[s, d], recv_sem=out_recv.at[s, d],
            device_id=(dst, ml), device_id_type=MESH)

    def out_arrival(s, d):
        src = lax.rem(me + W - d, W)
        return pltpu.make_async_remote_copy(
            src_ref=osend.at[block(me, s), src], dst_ref=out_ref.at[src * SL + block(me, s)],
            send_sem=out_send.at[s, d], recv_sem=out_recv.at[s, d],
            device_id=(src, ml), device_id_type=MESH)

    def lev_copy(s, d):
        dst = lax.rem(ml + d, NL)
        return pltpu.make_async_remote_copy(
            src_ref=lev_send.at[s, dst], dst_ref=lev_recv.at[s, ml],
            send_sem=lev_ssem.at[s, d], recv_sem=lev_rsem.at[s, d],
            device_id=(me, dst), device_id_type=MESH)

    def lev_arrival(s, d):
        src = lax.rem(ml + NL - d, NL)
        return pltpu.make_async_remote_copy(
            src_ref=lev_send.at[s, src], dst_ref=lev_recv.at[s, src],
            send_sem=lev_ssem.at[s, d], recv_sem=lev_rsem.at[s, d],
            device_id=(me, src), device_id_type=MESH)

    def own_in(s):
        return pltpu.make_async_copy(stage.at[me * SL + s], recv.at[s, me], own_sem.at[s])

    def own_out(s):
        return pltpu.make_async_copy(
            osend.at[block(me, s), me], out_ref.at[me * SL + block(me, s)], out_own.at[s])

    def flag_copy(d):
        dst = lax.rem(me + d, W)
        return pltpu.make_async_remote_copy(
            src_ref=flags.at[W], dst_ref=flags.at[me], send_sem=flag_send.at[d], recv_sem=flag_recv.at[d],
            device_id=(dst, ml), device_id_type=MESH)

    def flag_arrival(d):
        src = lax.rem(me + W - d, W)
        return pltpu.make_async_remote_copy(
            src_ref=flags.at[W], dst_ref=flags.at[src], send_sem=flag_send.at[d], recv_sem=flag_recv.at[d],
            device_id=(src, ml), device_id_type=MESH)

    def table_in(s):
        return pltpu.make_async_copy(tables_ref.at[s], tab.at[s], tab_sem.at[s])

    if compact:
        held_enough = jnp.float32(1)
        for s in range(0, SL, 2):
            even, odd = wave_ref[me * SL + s], wave_ref[me * SL + s + 1]
            late = jnp.where(even > odd, tile_ref[s], tile_ref[s + 1])
            held_enough = jnp.where(late * TILE >= H // 2, held_enough, jnp.float32(0))
        flags[W] = jnp.full(flags.shape[1:], held_enough)
        flags[me] = jnp.full(flags.shape[1:], held_enough)

    held_copy.wait()

    @pl.loop(0, waves)
    def _(s):
        wave = wave_ref[s]
        if compact:
            partner = wave_ref[s + 1 - 2 * (s % 2)]
            wave = jnp.where(halved(me), jnp.minimum(wave, partner), wave)
        stage[s] = held[wave]

    @pl.loop(0, SL)
    def _(s):
        @pl.when(full_turn(me, s, 0))
        def _():
            for d in order:
                in_copy(s, d).start()

        own_in(s).start()
        table_in(s).start()

    if compact:
        for d in order:
            flag_copy(d).start()

    rows = PAIR * LP * NL
    levels = LP * NL
    up = (iota((rows, levels), 0) // PAIR == iota((rows, levels), 1)).astype(jnp.float32)
    down = (iota((LP, C), 0) == iota((LP, C), 1) // FIELDS).astype(jnp.float32)
    wide = jnp.dot(
        lax.dot_general(up, coupling_ref[...], NT, precision=lax.Precision.HIGHEST), down,
        precision=lax.Precision.HIGHEST)
    kept = iota((rows, C), 1) % FIELDS == iota((rows, C), 0) % PAIR + FIRST
    k_high[...], k_low[...] = split(jnp.where(kept, wide, 0.0))
    er, ec = iota((C, rows), 0), iota((C, rows), 1) % (PAIR * LP)
    expand = ((er // FIELDS == ec // PAIR) & (er % FIELDS == ec % PAIR + FIRST)).astype(jnp.float32)
    expand = expand.astype(jnp.bfloat16)
    flip = (iota((TW, TW), 0) + iota((TW, TW), 1) == TW - 1).astype(jnp.float32).astype(jnp.bfloat16)

    def flipped(v):
        high, low = split(v)
        return mm(high, flip) + mm(low, flip)

    @pl.loop(0, SL)
    def _(s):
        wave = wave_ref[me * SL + s]
        first = tile_ref[s] * TILE
        m = (wave * N) // waves
        for d in order:
            @pl.when(full_turn(lax.rem(me + W - d, W), s, 0))
            def _():
                in_arrival(s, d).wait_recv()

        own_in(s).wait()
        table_in(s).wait()

        for t in range(nt):
            w_north = [t * BPT + b for b in range(BPT)]
            w_south = [half + w for w in w_north]
            north = jnp.concatenate([recv[s - s % 2 if halved(w) else s, w] for w in w_north], axis=1)
            south = jnp.concatenate([recv[s - s % 2 if halved(w) else s, w] for w in w_south], axis=1)
            south = flipped(south)
            for v, at, row in ((north, t, 0), (south, nt - 1 - t, C)):
                lanes = pl.ds(at * TW, TW)
                used = iota((1, TW), 1) + at * TW >= first
                scaled = v * jnp.where(used, gauss_ref[:, lanes], 0.0)
                high, low = split(scaled)
                x_high[pl.ds(row, C), lanes] = high
                x_low[pl.ds(row, C), lanes] = low

        @pl.loop(0, N // NW)
        def _(j):
            lanes = pl.ds(pl.multiple_of(j * NW, NW), NW)
            t_high, t_low = split(tab[s, :, lanes])
            f = mm3(x_high[...], x_low[...], t_high, t_low)
            degree = iota((1, NW), 1) + j * NW
            used = degree >= m
            sign = jnp.where((degree + m) % 2 == 0, 1.0, -1.0)
            spectral = jnp.where(used, f[:C] + sign * f[C:], 0.0)
            spec[:, lanes] = spectral
            s_high, s_low = split(spectral)
            part = mm3(k_high[...], k_low[...], s_high, s_low)
            for l in range(NL):
                lev_send[s, l, :, lanes] = part[l * PAIR * LP:(l + 1) * PAIR * LP]

        lev_recv[s, ml] = lev_send[s, ml]
        for d in lev_order:
            lev_copy(s, d).start()
        for d in lev_order:
            lev_arrival(s, d).wait_recv()

        @pl.loop(0, N // NW)
        def _(j):
            lanes = pl.ds(pl.multiple_of(j * NW, NW), NW)
            degree = iota((1, NW), 1) + j * NW
            sign = jnp.where((degree + m) % 2 == 0, 1.0, -1.0)
            factor = (degree * (degree + 1)).astype(jnp.float32) / float(N * (N - 1))
            p_high, p_low = split(jnp.concatenate([lev_recv[s, l, :, lanes] for l in range(NL)], axis=0))
            coupled = mm(expand, p_high) + mm(expand, p_low)
            updated = spec[:, lanes] - factor * coupled
            u_high, u_low = split(updated)
            r_high[pl.ds(0, C), lanes] = u_high
            r_low[pl.ds(0, C), lanes] = u_low
            w_high, w_low = split(sign * updated)
            r_high[pl.ds(C, C), lanes] = w_high
            r_low[pl.ds(C, C), lanes] = w_low

        @pl.loop(0, nt)
        def _(i):
            rows_here = pl.ds(pl.multiple_of(i * TW, TW), TW)
            t_high, t_low = split(tab[s, rows_here, :])
            o = mm3(r_high[...], r_low[...], t_high, t_low, NT)
            used = iota((1, TW), 1) + i * TW >= first
            o = jnp.where(used, o, 0.0)
            north = o[:C]
            south = flipped(o[C:])

            def store(at, add):
                for b in range(BPT):
                    cut = slice(b * LAT, (b + 1) * LAT)
                    for w, v in ((i * BPT + b, north), (half + (nt - 1 - i) * BPT + b, south)):
                        osend[at, w] = osend[at, w] + v[:, cut] if add else v[:, cut]

            if compact:
                second = (i < nt // 2) & (s % 2 == 1)

                @pl.when(second)
                def _():
                    store(s - 1, True)

                @pl.when(jnp.logical_not(second))
                def _():
                    store(s, False)
            else:
                store(s, False)

        for d in order:
            @pl.when(full_turn(lax.rem(me + d, W), s, 1))
            def _():
                out_copy(s, d).start()

        @pl.when(full_turn(me, s, 1))
        def _():
            own_out(s).start()

    @pl.loop(0, SL)
    def _(s):
        @pl.when(full_turn(me, s, 0))
        def _():
            for d in order:
                in_copy(s, d).wait_send()

        @pl.when(full_turn(me, s, 1))
        def _():
            own_out(s).wait()
            for d in order:
                out_arrival(s, d).wait_recv()

        for d in order:
            @pl.when(full_turn(lax.rem(me + d, W), s, 1))
            def _():
                out_copy(s, d).wait_send()

        for d in lev_order:
            lev_copy(s, d).wait_send()

    if compact:
        for d in order:
            flag_copy(d).wait_send()
            flag_arrival(d).wait_recv()
        flag_ref[...] = functools.reduce(jnp.minimum, [flags[w] for w in range(W)])
    else:
        flag_ref[...] = jnp.ones_like(flag_ref)


def transform(W, NL, compact, grid, legendre, gauss_weights, wave_of_slot, first_tile, coupling):
    waves, C, LAT = grid.shape
    SL, H, N = legendre.shape
    rows = PAIR * (C // FIELDS)
    f32, bf16, dma = jnp.float32, jnp.bfloat16, pltpu.SemaphoreType.DMA
    vmem = pl.BlockSpec(memory_space=pltpu.VMEM)
    smem = pl.BlockSpec(memory_space=pltpu.SMEM)
    hbm = pl.BlockSpec(memory_space=pl.ANY)
    return pl.pallas_call(
        functools.partial(spectral_kernel, W, NL, compact),
        out_shape=(
            jax.ShapeDtypeStruct((waves, C, LAT), f32), jax.ShapeDtypeStruct((8, 128), f32)),
        in_specs=[smem, smem, vmem, vmem, hbm, hbm],
        out_specs=(hbm, vmem),
        scratch_shapes=[
            pltpu.VMEM((waves, C, LAT), f32),
            pltpu.VMEM((waves, C, LAT), f32),
            pltpu.VMEM((SL, H, N), f32),
            pltpu.VMEM((SL, W, C, LAT), f32),
            pltpu.VMEM((SL, W, C, LAT), f32),
            pltpu.VMEM((SL, NL, rows, N), f32),
            pltpu.VMEM((SL, NL, rows, N), f32),
            pltpu.VMEM((2 * C, H), bf16),
            pltpu.VMEM((2 * C, H), bf16),
            pltpu.VMEM((C, N), f32),
            pltpu.VMEM((2 * C, N), bf16),
            pltpu.VMEM((2 * C, N), bf16),
            pltpu.VMEM((rows * NL, C), bf16),
            pltpu.VMEM((rows * NL, C), bf16),
            dma, dma((SL,)), dma((SL,)),
            dma((SL, W)), dma((SL, W)),
            dma((SL, NL)), dma((SL, NL)),
            dma((SL,)), dma((SL, W)), dma((SL, W)),
            pltpu.VMEM((W + 1, 8, 128), f32), dma((W,)), dma((W,)),
        ],
        compiler_params=pltpu.CompilerParams(
            collective_id=0 if compact else 1, has_side_effects=True, vmem_limit_bytes=VMEM_BYTES),
        name="spectral_half" if compact else "spectral",
    )(wave_of_slot, first_tile, gauss_weights[None, :], coupling.T, grid, legendre)


def solution(mesh):
    W, NL = mesh.shape["wave"], mesh.shape["lev"]

    def shards(grid_data, legendre, gauss_weights, wave_of_slot, first_tile, coupling):
        grid = jnp.transpose(grid_data, (1, 2, 0))
        rest = (grid, legendre, gauss_weights, wave_of_slot, first_tile, coupling)

        def everything():
            return unpack(W, False, wave_of_slot, transform(W, NL, False, *rest)[0])

        if W % 4 or legendre.shape[0] % 2:
            out = everything()
        else:
            back, flag = transform(W, NL, True, *rest)
            out = lax.cond(
                flag[0, 0] > 0.5, lambda: unpack(W, True, wave_of_slot, back), everything)
        return jnp.transpose(out, (2, 0, 1))

    placed = (P("wave", None, "lev"), P("wave", None, None), P(), P(), P("wave"), P(None, "lev"))
    return jax.shard_map(
        shards, mesh=mesh, in_specs=placed, out_specs=P("wave", None, "lev"), check_vma=False
    )
```

```python
import functools

import jax
import jax.numpy as jnp
from jax import lax
from jax.experimental import pallas as pl
from jax.experimental.pallas import tpu as pltpu
from jax.sharding import PartitionSpec as P

TILE = 128
FIELDS = 6
PAIR = 2
FIRST = 2
MESH = pl.DeviceIdType.MESH
NN = (((1,), (0,)), ((), ()))
NT = (((1,), (1,)), ((), ()))
VMEM_BYTES = 64 * 1024 * 1000


def mm(a, b, dims=NN):
    return lax.dot_general(a, b, dims, preferred_element_type=jnp.float32)


def split(v):
    high = v.astype(jnp.bfloat16)
    return high, (v - high.astype(jnp.float32)).astype(jnp.bfloat16)


def mm3(a_high, a_low, b_high, b_low, dims=NN):
    return mm(a_high, b_high, dims) + (mm(a_low, b_high, dims) + mm(a_high, b_low, dims))


def iota(shape, axis):
    return lax.broadcasted_iota(jnp.int32, shape, axis)


def polar(w, W):
    return (w < W // 4) | (w >= W - W // 4)


def unpack_kernel(W, compact, wave_ref, y_ref, out_ref, held, zero, in_sem, out_sem):
    waves = wave_ref.shape[0]
    halved = polar(lax.axis_index("wave"), W) if compact else False

    group = held.shape[0] // in_sem.shape[0]

    def fetch(g):
        span = pl.ds(g * group, group)
        return pltpu.make_async_copy(y_ref.at[span], held.at[span], in_sem.at[g])

    def put(s, src):
        return pltpu.make_async_copy(src, out_ref.at[wave_ref[s]], out_sem)

    for g in range(waves // group):
        fetch(g).start()
    if compact:
        zero[...] = jnp.zeros_like(zero)
    for g in range(waves // group):
        fetch(g).wait()
        for s in range(g * group, (g + 1) * group):
            if compact:
                even = s - s % 2
                empty = halved & (wave_ref[s] > wave_ref[even + 1 - s % 2])

                @pl.when(empty)
                def _():
                    put(s, zero).start()

                @pl.when(jnp.logical_not(empty))
                def _():
                    put(s, held.at[jnp.where(halved, even, s)]).start()
            else:
                put(s, held.at[s]).start()
    pltpu.make_async_copy(held, out_ref, out_sem).wait()


def unpack(W, compact, wave_of_slot, packed):
    waves = packed.shape[0]
    return pl.pallas_call(
        functools.partial(unpack_kernel, W, compact),
        out_shape=jax.ShapeDtypeStruct(packed.shape, jnp.float32),
        in_specs=[pl.BlockSpec(memory_space=pltpu.SMEM), pl.BlockSpec(memory_space=pl.ANY)],
        out_specs=pl.BlockSpec(memory_space=pl.ANY),
        scratch_shapes=[
            pltpu.VMEM(packed.shape, jnp.float32),
            pltpu.VMEM(packed.shape[1:], jnp.float32),
            pltpu.SemaphoreType.DMA((waves // 4 if waves % 4 == 0 else waves,)),
            pltpu.SemaphoreType.DMA,
        ],
        compiler_params=pltpu.CompilerParams(vmem_limit_bytes=VMEM_BYTES),
        name="unpack_half" if compact else "unpack",
    )(wave_of_slot, packed)


def spectral_kernel(
    W, NL, compact,
    wave_ref, tile_ref, gauss_ref, coupling_ref, grid_ref, tables_ref, out_ref, flag_ref,
    held, stage, tab, recv, osend, lev_send, lev_recv, x_high, x_low, spec, r_high, r_low, k_high, k_low,
    held_sem, tab_sem, own_sem, in_send, in_recv, lev_ssem, lev_rsem, out_own, out_send, out_recv,
    flags, flag_send, flag_recv,
):
    SL, H, N = tab.shape
    C, LAT = recv.shape[2], recv.shape[3]
    waves = wave_ref.shape[0]
    LP = C // FIELDS
    half = W // 2
    TW = max(256, LAT)
    BPT = TW // LAT
    nt = H // TW
    NW = 256
    me = lax.axis_index("wave")
    ml = lax.axis_index("lev")
    order = sorted(range(1, W), key=lambda d: (abs(d - half), d))
    lev_order = sorted(range(1, NL), key=lambda d: (abs(d - NL // 2), d))

    held_copy = pltpu.make_async_copy(grid_ref, held, held_sem)
    held_copy.start()
    def halved(w):
        return polar(w, W) if compact else False

    def full_turn(w, s, parity):
        return jnp.logical_not(halved(w)) | (s % 2 == parity) if compact else s >= 0

    def block(w, s):
        return jnp.where(halved(w), s - s % 2, s) if compact else s

    barrier = pltpu.get_barrier_semaphore()
    for d in range(1, W):
        pl.semaphore_signal(barrier, inc=1, device_id=(lax.rem(me + d, W), ml), device_id_type=MESH)
    for d in range(1, NL):
        pl.semaphore_signal(barrier, inc=1, device_id=(me, lax.rem(ml + d, NL)), device_id_type=MESH)
    pl.semaphore_wait(barrier, W - 1 + NL - 1)

    def in_copy(s, d):
        dst = lax.rem(me + d, W)
        return pltpu.make_async_remote_copy(
            src_ref=stage.at[dst * SL + s], dst_ref=recv.at[s, me],
            send_sem=in_send.at[s, d], recv_sem=in_recv.at[s, d],
            device_id=(dst, ml), device_id_type=MESH)

    def in_arrival(s, d):
        src = lax.rem(me + W - d, W)
        return pltpu.make_async_remote_copy(
            src_ref=stage.at[me * SL + s], dst_ref=recv.at[s, src],
            send_sem=in_send.at[s, d], recv_sem=in_recv.at[s, d],
            device_id=(src, ml), device_id_type=MESH)

    def out_copy(s, d):
        dst = lax.rem(me + d, W)
        return pltpu.make_async_remote_copy(
            src_ref=osend.at[block(dst, s), dst], dst_ref=out_ref.at[me * SL + block(dst, s)],
            send_sem=out_send.at[s, d], recv_sem=out_recv.at[s, d],
            device_id=(dst, ml), device_id_type=MESH)

    def out_arrival(s, d):
        src = lax.rem(me + W - d, W)
        return pltpu.make_async_remote_copy(
            src_ref=osend.at[block(me, s), src], dst_ref=out_ref.at[src * SL + block(me, s)],
            send_sem=out_send.at[s, d], recv_sem=out_recv.at[s, d],
            device_id=(src, ml), device_id_type=MESH)

    def lev_copy(s, d):
        dst = lax.rem(ml + d, NL)
        return pltpu.make_async_remote_copy(
            src_ref=lev_send.at[s, dst], dst_ref=lev_recv.at[s, ml],
            send_sem=lev_ssem.at[s, d], recv_sem=lev_rsem.at[s, d],
            device_id=(me, dst), device_id_type=MESH)

    def lev_arrival(s, d):
        src = lax.rem(ml + NL - d, NL)
        return pltpu.make_async_remote_copy(
            src_ref=lev_send.at[s, src], dst_ref=lev_recv.at[s, src],
            send_sem=lev_ssem.at[s, d], recv_sem=lev_rsem.at[s, d],
            device_id=(me, src), device_id_type=MESH)

    def own_in(s):
        return pltpu.make_async_copy(stage.at[me * SL + s], recv.at[s, me], own_sem.at[s])

    def own_out(s):
        return pltpu.make_async_copy(
            osend.at[block(me, s), me], out_ref.at[me * SL + block(me, s)], out_own.at[s])

    def flag_copy(d):
        dst = lax.rem(me + d, W)
        return pltpu.make_async_remote_copy(
            src_ref=flags.at[W], dst_ref=flags.at[me], send_sem=flag_send.at[d], recv_sem=flag_recv.at[d],
            device_id=(dst, ml), device_id_type=MESH)

    def flag_arrival(d):
        src = lax.rem(me + W - d, W)
        return pltpu.make_async_remote_copy(
            src_ref=flags.at[W], dst_ref=flags.at[src], send_sem=flag_send.at[d], recv_sem=flag_recv.at[d],
            device_id=(src, ml), device_id_type=MESH)

    def table_in(s):
        return pltpu.make_async_copy(tables_ref.at[s], tab.at[s], tab_sem.at[s])

    if compact:
        held_enough = jnp.float32(1)
        for s in range(0, SL, 2):
            even, odd = wave_ref[me * SL + s], wave_ref[me * SL + s + 1]
            late = jnp.where(even > odd, tile_ref[s], tile_ref[s + 1])
            held_enough = jnp.where(late * TILE >= H // 2, held_enough, jnp.float32(0))
        flags[W] = jnp.full(flags.shape[1:], held_enough)
        flags[me] = jnp.full(flags.shape[1:], held_enough)

    held_copy.wait()

    @pl.loop(0, waves)
    def _(s):
        wave = wave_ref[s]
        if compact:
            partner = wave_ref[s + 1 - 2 * (s % 2)]
            wave = jnp.where(halved(me), jnp.minimum(wave, partner), wave)
        stage[s] = held[wave]

    @pl.loop(0, SL)
    def _(s):
        @pl.when(full_turn(me, s, 0))
        def _():
            for d in order:
                in_copy(s, d).start()

        own_in(s).start()
        table_in(s).start()

    if compact:
        for d in order:
            flag_copy(d).start()

    rows = PAIR * LP * NL
    levels = LP * NL
    up = (iota((rows, levels), 0) // PAIR == iota((rows, levels), 1)).astype(jnp.float32)
    down = (iota((LP, C), 0) == iota((LP, C), 1) // FIELDS).astype(jnp.float32)
    wide = jnp.dot(
        lax.dot_general(up, coupling_ref[...], NT, precision=lax.Precision.HIGHEST), down,
        precision=lax.Precision.HIGHEST)
    kept = iota((rows, C), 1) % FIELDS == iota((rows, C), 0) % PAIR + FIRST
    k_high[...], k_low[...] = split(jnp.where(kept, wide, 0.0))
    er, ec = iota((C, rows), 0), iota((C, rows), 1) % (PAIR * LP)
    expand = ((er // FIELDS == ec // PAIR) & (er % FIELDS == ec % PAIR + FIRST)).astype(jnp.float32)
    expand = expand.astype(jnp.bfloat16)
    flip = (iota((TW, TW), 0) + iota((TW, TW), 1) == TW - 1).astype(jnp.float32).astype(jnp.bfloat16)

    def flipped(v):
        high, low = split(v)
        return mm(high, flip) + mm(low, flip)

    @pl.loop(0, SL)
    def _(s):
        wave = wave_ref[me * SL + s]
        first = tile_ref[s] * TILE
        m = (wave * N) // waves
        for d in order:
            @pl.when(full_turn(lax.rem(me + W - d, W), s, 0))
            def _():
                in_arrival(s, d).wait_recv()

        own_in(s).wait()
        table_in(s).wait()

        for t in range(nt):
            w_north = [t * BPT + b for b in range(BPT)]
            w_south = [half + w for w in w_north]
            north = jnp.concatenate([recv[s - s % 2 if halved(w) else s, w] for w in w_north], axis=1)
            south = jnp.concatenate([recv[s - s % 2 if halved(w) else s, w] for w in w_south], axis=1)
            south = flipped(south)
            for v, at, row in ((north, t, 0), (south, nt - 1 - t, C)):
                lanes = pl.ds(at * TW, TW)
                used = iota((1, TW), 1) + at * TW >= first
                scaled = v * jnp.where(used, gauss_ref[:, lanes], 0.0)
                high, low = split(scaled)
                x_high[pl.ds(row, C), lanes] = high
                x_low[pl.ds(row, C), lanes] = low

        @pl.loop(0, N // NW)
        def _(j):
            lanes = pl.ds(pl.multiple_of(j * NW, NW), NW)
            t_high, t_low = split(tab[s, :, lanes])
            f = mm3(x_high[...], x_low[...], t_high, t_low)
            degree = iota((1, NW), 1) + j * NW
            used = degree >= m
            sign = jnp.where((degree + m) % 2 == 0, 1.0, -1.0)
            spectral = jnp.where(used, f[:C] + sign * f[C:], 0.0)
            spec[:, lanes] = spectral
            s_high, s_low = split(spectral)
            part = mm3(k_high[...], k_low[...], s_high, s_low)
            for l in range(NL):
                lev_send[s, l, :, lanes] = part[l * PAIR * LP:(l + 1) * PAIR * LP]

        lev_recv[s, ml] = lev_send[s, ml]
        for d in lev_order:
            lev_copy(s, d).start()
        for d in lev_order:
            lev_arrival(s, d).wait_recv()

        @pl.loop(0, N // NW)
        def _(j):
            lanes = pl.ds(pl.multiple_of(j * NW, NW), NW)
            degree = iota((1, NW), 1) + j * NW
            sign = jnp.where((degree + m) % 2 == 0, 1.0, -1.0)
            factor = (degree * (degree + 1)).astype(jnp.float32) / float(N * (N - 1))
            p_high, p_low = split(jnp.concatenate([lev_recv[s, l, :, lanes] for l in range(NL)], axis=0))
            coupled = mm(expand, p_high) + mm(expand, p_low)
            updated = spec[:, lanes] - factor * coupled
            u_high, u_low = split(updated)
            r_high[pl.ds(0, C), lanes] = u_high
            r_low[pl.ds(0, C), lanes] = u_low
            w_high, w_low = split(sign * updated)
            r_high[pl.ds(C, C), lanes] = w_high
            r_low[pl.ds(C, C), lanes] = w_low

        @pl.loop(0, nt)
        def _(i):
            rows_here = pl.ds(pl.multiple_of(i * TW, TW), TW)
            t_high, t_low = split(tab[s, rows_here, :])
            o = mm3(r_high[...], r_low[...], t_high, t_low, NT)
            used = iota((1, TW), 1) + i * TW >= first
            o = jnp.where(used, o, 0.0)
            north = o[:C]
            south = flipped(o[C:])

            def store(at, add):
                for b in range(BPT):
                    cut = slice(b * LAT, (b + 1) * LAT)
                    for w, v in ((i * BPT + b, north), (half + (nt - 1 - i) * BPT + b, south)):
                        osend[at, w] = osend[at, w] + v[:, cut] if add else v[:, cut]

            if compact:
                second = (i < nt // 2) & (s % 2 == 1)

                @pl.when(second)
                def _():
                    store(s - 1, True)

                @pl.when(jnp.logical_not(second))
                def _():
                    store(s, False)
            else:
                store(s, False)

        for d in order:
            @pl.when(full_turn(lax.rem(me + d, W), s, 1))
            def _():
                out_copy(s, d).start()

        @pl.when(full_turn(me, s, 1))
        def _():
            own_out(s).start()

    @pl.loop(0, SL)
    def _(s):
        @pl.when(full_turn(me, s, 0))
        def _():
            for d in order:
                in_copy(s, d).wait_send()

        @pl.when(full_turn(me, s, 1))
        def _():
            own_out(s).wait()
            for d in order:
                out_arrival(s, d).wait_recv()

        for d in order:
            @pl.when(full_turn(lax.rem(me + d, W), s, 1))
            def _():
                out_copy(s, d).wait_send()

        for d in lev_order:
            lev_copy(s, d).wait_send()

    if compact:
        for d in order:
            flag_copy(d).wait_send()
            flag_arrival(d).wait_recv()
        flag_ref[...] = functools.reduce(jnp.minimum, [flags[w] for w in range(W)])
    else:
        flag_ref[...] = jnp.ones_like(flag_ref)


def transform(W, NL, compact, grid, legendre, gauss_weights, wave_of_slot, first_tile, coupling):
    waves, C, LAT = grid.shape
    SL, H, N = legendre.shape
    rows = PAIR * (C // FIELDS)
    f32, bf16, dma = jnp.float32, jnp.bfloat16, pltpu.SemaphoreType.DMA
    vmem = pl.BlockSpec(memory_space=pltpu.VMEM)
    smem = pl.BlockSpec(memory_space=pltpu.SMEM)
    hbm = pl.BlockSpec(memory_space=pl.ANY)
    return pl.pallas_call(
        functools.partial(spectral_kernel, W, NL, compact),
        out_shape=(
            jax.ShapeDtypeStruct((waves, C, LAT), f32), jax.ShapeDtypeStruct((8, 128), f32)),
        in_specs=[smem, smem, vmem, vmem, hbm, hbm],
        out_specs=(hbm, vmem),
        scratch_shapes=[
            pltpu.VMEM((waves, C, LAT), f32),
            pltpu.VMEM((waves, C, LAT), f32),
            pltpu.VMEM((SL, H, N), f32),
            pltpu.VMEM((SL, W, C, LAT), f32),
            pltpu.VMEM((SL, W, C, LAT), f32),
            pltpu.VMEM((SL, NL, rows, N), f32),
            pltpu.VMEM((SL, NL, rows, N), f32),
            pltpu.VMEM((2 * C, H), bf16),
            pltpu.VMEM((2 * C, H), bf16),
            pltpu.VMEM((C, N), f32),
            pltpu.VMEM((2 * C, N), bf16),
            pltpu.VMEM((2 * C, N), bf16),
            pltpu.VMEM((rows * NL, C), bf16),
            pltpu.VMEM((rows * NL, C), bf16),
            dma, dma((SL,)), dma((SL,)),
            dma((SL, W)), dma((SL, W)),
            dma((SL, NL)), dma((SL, NL)),
            dma((SL,)), dma((SL, W)), dma((SL, W)),
            pltpu.VMEM((W + 1, 8, 128), f32), dma((W,)), dma((W,)),
        ],
        compiler_params=pltpu.CompilerParams(
            collective_id=0 if compact else 1, has_side_effects=True, vmem_limit_bytes=VMEM_BYTES),
        name="spectral_half" if compact else "spectral",
    )(wave_of_slot, first_tile, gauss_weights[None, :], coupling.T, grid, legendre)


def solution(mesh):
    W, NL = mesh.shape["wave"], mesh.shape["lev"]

    def shards(grid_data, legendre, gauss_weights, wave_of_slot, first_tile, coupling):
        grid = jnp.transpose(grid_data, (1, 2, 0))
        rest = (grid, legendre, gauss_weights, wave_of_slot, first_tile, coupling)

        def everything():
            return unpack(W, False, wave_of_slot, transform(W, NL, False, *rest)[0])

        if W % 4 or legendre.shape[0] % 2:
            out = everything()
        else:
            back, flag = transform(W, NL, True, *rest)
            out = lax.cond(
                flag[0, 0] > 0.5, lambda: unpack(W, True, wave_of_slot, back), everything)
        return jnp.transpose(out, (2, 0, 1))

    placed = (P("wave", None, "lev"), P("wave", None, None), P(), P(), P("wave"), P(None, "lev"))
    return jax.shard_map(
        shards, mesh=mesh, in_specs=placed, out_specs=P("wave", None, "lev"), check_vma=False
    )
```
